32 devices in a mesh: parts: 2 (over x), space: 16 (over z, y, core).
Axes of the slice: x: 2, y: 2, z: 4, core: 2. Of those that a mesh axis runs over, the one named last changes fastest.
Arguments:
- observed: bfloat16 [128, 4096, 128], P(('parts', 'space')), parts along dimension 0, may hold values from -6 to 6
- weights: bfloat16 [128, 4096, 128], P(('parts', 'space')), parts along dimension 0, may hold values from 0 to 1, as said below
- pixel_factors: float32 [128, 16, 4096], P(('parts', 'space')), parts along dimension 0, may hold values from -6 to 6
- pixel_bias: float32 [128, 4096], P(('parts', 'space')), parts along dimension 0, may hold values from -4 to 4
- date_factors: float32 [32, 128], P('parts'), parts along dimension 0, may hold values from -1.5 to 1.5
- date_bias: float32 [256], P('parts'), parts along dimension 0, may hold values from -4 to 4
- land_class: int32 [128, 4096], P(('parts', 'space')), parts along dimension 0, may hold values from 0 to 3
- conductance: float32 [4], replicated, may hold values from 0.3 to 3
Outputs:
- grad_pixel_factors: float32 [128, 16, 4096], P(('parts', 'space')), parts along dimension 0
- grad_pixel_bias: float32 [128, 4096], P(('parts', 'space')), parts along dimension 0
- grad_date_factors: float32 [32, 128], P('parts'), parts along dimension 0
- grad_date_bias: float32 [256], P('parts'), parts along dimension 0
The draws below stay inside these ranges and needn't reach their ends.
There are 2 independent parts, one for each index of `parts`. The reference program is written for one: setup_inputs(seed, part) draws one part's arguments, and reference() takes and returns one part's arrays. A program takes and returns all parts, laid end to end along the dimension named above; an argument that names none is the same for every part. Nothing has to cross between parts.
Inputs may be any that keep to these rules, and one draw needn't show every extreme that they name: Every pixel has a nonzero weight on at least one date; nonzero weights are 0.5 or more.
All inputs are finite; a program needn't handle non-finite values.
Results may differ from the reference program's by a relative error of at most 0.0003.
Values sent between devices are 32-bit elements; how exact they have to be, the bound alone decides.
A program may use at most 64 MiB of HBM per device.

```python
import math
import jax
import jax.numpy as jnp
from jax import lax

RANK = 16
COLS = 4096
DATES = 128
CLASSES = 4
ROWS = 64
PIXELS = 262144


def draw_weights(key, part):
    first, second, third = jax.random.split(jax.random.fold_in(key, 11), 3)
    position = jnp.arange(ROWS, dtype=jnp.float32) / max(ROWS - 1, 1)
    chance = 0.2 + 0.4 * position
    level = jax.random.uniform(third, (ROWS, COLS, DATES), jnp.float32, 0.5, 1.0)
    draws = jax.random.uniform(first, (ROWS, COLS, DATES), jnp.float32)
    forced = jax.random.randint(second, (ROWS, COLS, 1), 0, DATES)
    clear = (draws < chance[:, None, None]) | (jnp.arange(DATES)[None, None, :] == forced)
    return jnp.where(clear, level, jnp.float32(0.0)).astype(jnp.bfloat16)


def place_ends(array, stream_key, low, largest):
    longest = array.shape.index(max(array.shape))
    spots = []
    for shift in (0, 1):
        where = [jax.random.randint(jax.random.fold_in(stream_key, axis), (), 0, length) for axis, length in enumerate(array.shape)]
        where[longest] = (where[longest] + shift) % array.shape[longest]
        spots.append(tuple(where))
    return array.at[spots[0]].set(low).at[spots[1]].set(largest)


def block_levels(key, shape, pieces, smallest, high):
    def one(dim, parts):
        steps = jax.random.uniform(jax.random.fold_in(jax.random.fold_in(key, 6), dim), (parts,), jnp.float32, smallest / len(pieces), high / len(pieces))
        return jnp.repeat(jnp.exp(steps), shape[dim] // parts).reshape((-1,) + (1,) * (len(shape) - dim - 1))

    level = one(*pieces[0])
    for cut in pieces[1:]:
        level = level * one(*cut)
    return level


def gaussian(own_key, extent, spread, limit, cuts=(), held_as=jnp.bfloat16):
    loudness = block_levels(own_key, extent, cuts, -0.22, 0.18) if cuts else 1.0
    entries = jax.random.normal(own_key, extent, jnp.float32) * spread * loudness
    return jnp.minimum(jnp.maximum(entries, -limit), limit).astype(held_as)


def setup_inputs(seed: int = 0, part: int = 0) -> dict:
    seeds = jax.random.split(jax.random.key(seed), 9)
    part_keys = jax.random.split(jax.random.fold_in(seeds[8], part), 9)
    return {
        "observed": gaussian(part_keys[0], (ROWS, COLS, DATES), 1.0, 6.0, ((0, 16),)),
        "weights": draw_weights(jax.random.fold_in(jax.random.fold_in(seeds[8], part), 71), part),
        "pixel_factors": gaussian(part_keys[2], (ROWS, RANK, COLS), 1.0, 6.0, ((0, 16),), jnp.float32),
        "pixel_bias": gaussian(part_keys[3], (ROWS, COLS), 0.5, 4.0, ((0, 16),), jnp.float32),
        "date_factors": gaussian(part_keys[4], (RANK, DATES), RANK ** -0.5, 1.5, (), jnp.float32),
        "date_bias": gaussian(part_keys[5], (DATES,), 0.5, 4.0, (), jnp.float32),
        "land_class": place_ends(jax.random.randint(part_keys[6], (ROWS, COLS), 0, CLASSES), jax.random.fold_in(part_keys[6], 1), 0, CLASSES - 1).astype(jnp.int32),
        "conductance": jnp.clip(jnp.exp(jax.random.uniform(seeds[7], (CLASSES,), jnp.float32, math.log(0.3), math.log(3.0))), 0.3, 3.0),
    }


def lookup(land_class, conductance):
    cond = jnp.zeros(land_class.shape, jnp.float32)
    for klass in range(CLASSES):
        cond = cond + jnp.where(land_class == klass, conductance[klass], jnp.float32(0.0))
    return cond


def reference(observed, weights, pixel_factors, pixel_bias, date_factors, date_bias, land_class, conductance):
    count = jnp.sum(weights, dtype=jnp.float32)
    scale = jnp.float32(PIXELS) / count
    cond = lookup(land_class, conductance)
    weighted = cond[:, None, :] * pixel_factors
    stacked = jnp.concatenate([weighted, cond[:, None, :]], axis=1)
    padded = jnp.pad(stacked, ((1, 1), (0, 0), (1, 1)))
    beside_all = padded[:-2, :, 1:-1] + padded[2:, :, 1:-1] + padded[1:-1, :, :-2] + padded[1:-1, :, 2:]
    smooth = cond[:, None, :] * (beside_all[:, RANK:RANK + 1, :] * pixel_factors - beside_all[:, :RANK, :])
    block = math.gcd(ROWS, 16)
    blocks = ROWS // block
    hi = lax.Precision.HIGHEST

    def step(carry, items):
        obs, wts, fac, bias = items
        pred = jnp.einsum("yrw,rt->ywt", fac, date_factors, precision=hi) + bias[:, :, None] + date_bias
        resid = scale * wts.astype(jnp.float32) * (pred - obs.astype(jnp.float32))
        gfac = carry[0] + jnp.einsum("ywt,yrw->rt", resid, fac, precision=hi)
        gbias = carry[1] + jnp.sum(resid, axis=(0, 1))
        gpix = jnp.einsum("ywt,rt->yrw", resid, date_factors, precision=hi)
        return (gfac, gbias), (gpix, jnp.sum(resid, axis=2))

    items = (observed.reshape(blocks, block, COLS, DATES), weights.reshape(blocks, block, COLS, DATES),
             pixel_factors.reshape(blocks, block, RANK, COLS), pixel_bias.reshape(blocks, block, COLS))
    init = (jnp.zeros((RANK, DATES), jnp.float32), jnp.zeros((DATES,), jnp.float32))
    (gfac, gbias), (gpix, gpb) = lax.scan(step, init, items)
    grad_pixel_factors = gpix.reshape(ROWS, RANK, COLS) + smooth
    return grad_pixel_factors, gpb.reshape(ROWS, COLS), gfac, gbias
```

```python
import functools

import jax
import jax.numpy as jnp
from jax import lax
from jax.experimental import pallas as pl
from jax.experimental.pallas import tpu as pltpu
from jax.sharding import PartitionSpec as P

CLASSES = 4
CHUNK = 1024
MIB = 1024 * 1024


def split(x):
    head = x.astype(jnp.bfloat16)
    return head, (x - head.astype(jnp.float32)).astype(jnp.bfloat16)


def lookup(land_class, cond_ref):
    cond = jnp.zeros(land_class.shape, jnp.float32)
    for klass in range(CLASSES):
        cond = cond + jnp.where(land_class == klass, cond_ref[klass], jnp.float32(0.0))
    return cond


def beside(x):
    cols = x.shape[1]
    col = lax.broadcasted_iota(jnp.int32, x.shape, 1)
    left = jnp.where(col == 0, 0.0, pltpu.roll(x, 1, 1))
    right = jnp.where(col == cols - 1, 0.0, pltpu.roll(x, cols - 1, 1))
    return left + right


def kernel(
    n, group, chunk,
    cond_ref, obs_hbm, wts_hbm, fac_hbm, pb_hbm, df_ref, db_ref, lc_hbm,
    u_hbm, s_hbm, g_ref, gdf_ref, gdb_ref, scale_ref,
    obs, wts, fac, pb, lc, unscaled, smooth, halo_f, halo_c, rhs, back, stage_a, stage_b, cond,
    obs_sem, wts_sem, fac_sem, small_sem, u_sem, s_sem,
    halo_send, halo_recv, a_send, a_recv, b_send, b_recv,
):
    rows, rank, cols = fac.shape
    dates = obs.shape[2]
    per_row = cols // chunk
    steps = rows * per_row
    half = chunk // 2
    groups = n // group
    f32, bf16 = jnp.float32, jnp.bfloat16

    me = lax.axis_index("space")
    above = lax.rem(me + n - 1, n)
    below = lax.rem(me + 1, n)
    mine_a = lax.rem(me, group)
    mine_b = me // group
    peers_a = [mine_b * group + lax.rem(mine_a + k, group) for k in range(1, group)]
    peers_b = [lax.rem(mine_b + k, groups) * group + mine_a for k in range(1, groups)]

    barrier = pltpu.get_barrier_semaphore()
    greeted = [above, below] + peers_a + peers_b
    for peer in greeted:
        pl.semaphore_signal(
            barrier, inc=1, device_id={"space": peer}, device_id_type=pl.DeviceIdType.MESH
        )

    def chunk_copies(y, c, step):
        at = pl.ds(pl.multiple_of(c * chunk, chunk), chunk)
        return (
            pltpu.make_async_copy(obs_hbm.at[y, at], obs.at[y, at], obs_sem.at[step]),
            pltpu.make_async_copy(wts_hbm.at[y, at], wts.at[y, at], wts_sem.at[step]),
        )

    pb_copy = pltpu.make_async_copy(pb_hbm, pb, small_sem.at[0])
    lc_copy = pltpu.make_async_copy(lc_hbm, lc, small_sem.at[1])
    fac_copies = [
        pltpu.make_async_copy(fac_hbm.at[y], fac.at[y], fac_sem.at[y]) for y in range(rows)
    ]
    pb_copy.start()
    fac_copies[0].start()
    for y in range(rows):
        for c in range(per_row):
            for copy in chunk_copies(y, c, y * per_row + c):
                copy.start()
        if y + 1 < rows:
            fac_copies[y + 1].start()
    lc_copy.start()

    dh, dl = split(df_ref[...])
    bh, bl = split(db_ref[...])
    line = lax.broadcasted_iota(jnp.int32, (16, dates), 0)
    tail = jnp.where(
        line < 2, 1.0,
        jnp.where(line == 2, bh.astype(f32), jnp.where(line == 3, bl.astype(f32), 0.0)),
    ).astype(bf16)
    one = jnp.concatenate([dh, dh, dl, tail], axis=0)
    none = jnp.zeros_like(one)
    rhs[...] = jnp.concatenate(
        [jnp.concatenate([one, none], axis=1), jnp.concatenate([none, one], axis=1)], axis=0
    )
    ones_line = jnp.where(line == 0, 1.0, 0.0).astype(bf16)
    back[...] = jnp.concatenate(
        [
            jnp.concatenate([dh, dh], axis=1),
            jnp.concatenate([dl, jnp.zeros_like(dl)], axis=1),
            jnp.concatenate([ones_line, ones_line], axis=1),
        ],
        axis=0,
    )

    pl.semaphore_wait(barrier, len(greeted))

    def remote(src, dst, send, recv, peer):
        return pltpu.make_async_remote_copy(
            src_ref=src, dst_ref=dst, send_sem=send, recv_sem=recv,
            device_id={"space": peer}, device_id_type=pl.DeviceIdType.MESH,
        )

    halo = [
        remote(fac_hbm.at[0], halo_f.at[1], halo_send.at[0], halo_recv.at[0], above),
        remote(fac_hbm.at[rows - 1], halo_f.at[0], halo_send.at[1], halo_recv.at[1], below),
        remote(lc_hbm, halo_c.at[1], halo_send.at[2], halo_recv.at[2], above),
        remote(lc_hbm, halo_c.at[0], halo_send.at[3], halo_recv.at[3], below),
    ]
    for copy in halo:
        copy.start()
    pb_copy.wait()

    slot = lax.broadcasted_iota(jnp.int32, (16, chunk), 0)

    def u_copy(y, c, step):
        at = pl.ds(pl.multiple_of(c * chunk, chunk), chunk)
        return pltpu.make_async_copy(unscaled.at[y, :, at], u_hbm.at[y, :, at], u_sem.at[step])

    def body(y, c, carry):
        total, count = carry
        step = y * per_row + c
        for copy in chunk_copies(y, c, step):
            copy.wait()
        start = pl.multiple_of(c * chunk, chunk)
        fh, fl = split(fac[y, :, pl.ds(start, chunk)])
        ph, plow = split(pb[pl.ds(y, 1), pl.ds(start, chunk)])
        extra = jnp.where(
            slot == 0, ph.astype(f32),
            jnp.where(slot == 1, plow.astype(f32), jnp.where(slot < 4, 1.0, 0.0)),
        ).astype(bf16)
        lhs = jnp.concatenate([fh, fl, fh, extra], axis=0)
        halves = [lhs[:, :half], lhs[:, half:]]
        pred = lax.dot_general(
            jnp.concatenate(halves, axis=0), rhs[...], (((0,), (0,)), ((), ())),
            preferred_element_type=f32,
        )
        for j in range(2):
            at = pl.ds(pl.multiple_of(start + j * half, half), half)
            w = wts[y, at, :].astype(f32)
            count = count + jnp.sum(w.reshape(half // 8, 8, dates), axis=0)
            misfit = w * (pred[:, j * dates : (j + 1) * dates] - obs[y, at, :].astype(f32))
            mh, ml = split(misfit)
            both = jnp.concatenate([mh, ml], axis=1)
            total = total + lax.dot_general(
                halves[j], both, (((1,), (0,)), ((), ())), preferred_element_type=f32
            )
            pix = lax.dot_general(
                back[...], both, (((1,), (1,)), ((), ())), preferred_element_type=f32
            )
            unscaled[y, :, at] = pix[:rank] + pix[rank : 2 * rank]
            g_ref[pl.ds(y, 1), at] = pix[2 * rank : 2 * rank + 1]
        u_copy(y, c, step).start()
        return total, count

    carry = (jnp.zeros((64, 2 * dates), f32), jnp.zeros((8, dates), f32))
    for y in range(rows):
        fac_copies[y].wait()
        carry = lax.fori_loop(0, per_row, functools.partial(body, y), carry)
    total, count = carry

    gdf = total[:rank, :dates] + total[:rank, dates:] + total[rank : 2 * rank, :dates]
    gdb = total[50:51, :dates] + total[50:51, dates:]
    line8 = lax.broadcasted_iota(jnp.int32, (8, dates), 0)
    last = jnp.where(
        line8 == 0, gdb, jnp.where(line8 == 1, jnp.sum(count, axis=0, keepdims=True), 0.0)
    )
    stage_a[mine_a] = jnp.concatenate([gdf, last], axis=0)
    sends_a = [
        remote(stage_a.at[mine_a], stage_a.at[mine_a], a_send.at[k], a_recv.at[k], peer)
        for k, peer in enumerate(peers_a)
    ]
    for copy in sends_a:
        copy.start()

    lc_copy.wait()
    for copy in halo:
        copy.wait()
    cond[0:1] = jnp.where(me == 0, 0.0, lookup(halo_c[0, rows - 1 : rows, :], cond_ref))
    cond[rows + 1 : rows + 2] = jnp.where(me == n - 1, 0.0, lookup(halo_c[1, 0:1, :], cond_ref))
    cond[1 : rows + 1] = lookup(lc[...], cond_ref)

    def row_factors(y):
        return halo_f[0] if y < 0 else halo_f[1] if y == rows else fac[y]

    def smooth_row(y):
        own = cond[y + 1 : y + 2]
        north, south = cond[y : y + 1], cond[y + 2 : y + 3]
        f = fac[y]
        around = north + south + beside(own)
        weighted = north * row_factors(y - 1) + south * row_factors(y + 1) + beside(own * f)
        smooth[y] = own * (around * f - weighted)
        copy = pltpu.make_async_copy(smooth.at[y], s_hbm.at[y], s_sem.at[y])
        copy.start()
        return copy

    s_copies = [smooth_row(y) for y in range(rows // 2)]

    for copy in sends_a:
        copy.wait()
    part = stage_a[0]
    for k in range(1, group):
        part = part + stage_a[k]
    stage_b[mine_b] = part
    sends_b = [
        remote(stage_b.at[mine_b], stage_b.at[mine_b], b_send.at[k], b_recv.at[k], peer)
        for k, peer in enumerate(peers_b)
    ]
    for copy in sends_b:
        copy.start()

    s_copies += [smooth_row(y) for y in range(rows // 2, rows)]

    for copy in sends_b:
        copy.wait()
    part = stage_b[0]
    for k in range(1, groups):
        part = part + stage_b[k]
    clear = jnp.sum(part[rank + 1 : rank + 2], axis=1, keepdims=True)
    scale = jnp.float32(n * rows * cols) / clear
    gdf_ref[...] = scale * part[:rank]
    gdb_ref[...] = scale * part[rank : rank + 1]
    scale_ref[...] = jnp.broadcast_to(scale, scale_ref.shape)

    for y in range(rows):
        for c in range(per_row):
            u_copy(y, c, y * per_row + c).wait()
    for copy in s_copies:
        copy.wait()


def on_device(
    observed, weights, pixel_factors, pixel_bias, date_factors, date_bias, land_class, conductance
):
    rows, rank, cols = pixel_factors.shape
    dates = observed.shape[2]
    n = lax.axis_size("space")
    group = max(d for d in range(1, n + 1) if n % d == 0 and d * d <= n)
    groups = n // group
    chunk = min(CHUNK, cols)
    steps = rows * (cols // chunk)
    f32, bf16 = jnp.float32, jnp.bfloat16
    dma = pltpu.SemaphoreType.DMA
    hbm = pl.BlockSpec(memory_space=pl.ANY)
    vmem = pl.BlockSpec(memory_space=pltpu.VMEM)
    u, s, g, gdf, gdb, scale = pl.pallas_call(
        functools.partial(kernel, n, group, chunk),
        out_shape=(
            jax.ShapeDtypeStruct((rows, rank, cols), f32),
            jax.ShapeDtypeStruct((rows, rank, cols), f32),
            jax.ShapeDtypeStruct((rows, cols), f32),
            jax.ShapeDtypeStruct((rank, dates), f32),
            jax.ShapeDtypeStruct((1, dates), f32),
            jax.ShapeDtypeStruct((8, 128), f32),
        ),
        in_specs=[
            pl.BlockSpec(memory_space=pltpu.SMEM), hbm, hbm, hbm, hbm, vmem, vmem, hbm,
        ],
        out_specs=(hbm, hbm, vmem, vmem, vmem, vmem),
        scratch_shapes=[
            pltpu.VMEM((rows, cols, dates), bf16),
            pltpu.VMEM((rows, cols, dates), bf16),
            pltpu.VMEM((rows, rank, cols), f32),
            pltpu.VMEM((rows, cols), f32),
            pltpu.VMEM((rows, cols), jnp.int32),
            pltpu.VMEM((rows, rank, cols), f32),
            pltpu.VMEM((rows, rank, cols), f32),
            pltpu.VMEM((2, rank, cols), f32),
            pltpu.VMEM((2, rows, cols), jnp.int32),
            pltpu.VMEM((128, 2 * dates), bf16),
            pltpu.VMEM((48, 2 * dates), bf16),
            pltpu.VMEM((group, 24, dates), f32),
            pltpu.VMEM((groups, 24, dates), f32),
            pltpu.VMEM((rows + 2, cols), f32),
            dma((steps,)), dma((steps,)), dma((rows,)), dma((2,)), dma((steps,)), dma((rows,)),
            dma((4,)), dma((4,)),
            dma((group,)), dma((group,)), dma((groups,)), dma((groups,)),
        ],
        compiler_params=pltpu.CompilerParams(
            collective_id=0, has_side_effects=True, vmem_limit_bytes=40 * MIB
        ),
        name="gap_fill",
    )(
        conductance, observed, weights, pixel_factors, pixel_bias, date_factors,
        date_bias.reshape(1, dates), land_class,
    )
    scale = scale[0, 0]
    return scale * u + s, scale * g, gdf, gdb.reshape(dates)


def solution(mesh):
    return jax.shard_map(
        on_device,
        mesh=mesh,
        in_specs=(
            P(("parts", "space"), None, None),
            P(("parts", "space"), None, None),
            P(("parts", "space"), None, None),
            P(("parts", "space"), None),
            P("parts", None),
            P("parts"),
            P(("parts", "space"), None),
            P(),
        ),
        out_specs=(
            P(("parts", "space"), None, None),
            P(("parts", "space"), None),
            P("parts", None),
            P("parts"),
        ),
        check_vma=False,
    )
```

```python
import functools

import jax
import jax.numpy as jnp
from jax import lax
from jax.experimental import pallas as pl
from jax.experimental.pallas import tpu as pltpu
from jax.sharding import PartitionSpec as P

CLASSES = 4
CHUNK = 1024
GRANT = 44 * 1024 * 1024


def split(x):
    head = x.astype(jnp.bfloat16)
    return head, (x - head.astype(jnp.float32)).astype(jnp.bfloat16)


def lookup(land_class, cond_ref):
    cond = jnp.zeros(land_class.shape, jnp.float32)
    for klass in range(CLASSES):
        cond = cond + jnp.where(land_class == klass, cond_ref[klass], jnp.float32(0.0))
    return cond


def beside(x):
    cols = x.shape[1]
    col = lax.broadcasted_iota(jnp.int32, x.shape, 1)
    left = jnp.where(col == 0, 0.0, pltpu.roll(x, 1, 1))
    right = jnp.where(col == cols - 1, 0.0, pltpu.roll(x, cols - 1, 1))
    return left + right


def kernel(
    n, group, chunk,
    cond_hbm, obs_hbm, wts_hbm, fac_hbm, pb_hbm, df_hbm, db_hbm, lc_hbm,
    gpf_ref, gpb_ref, gdf_ref, gdb_ref,
    cond_ref, df_ref, db_ref,
    obs, wts, fac, pb, lc, smooth, halo_f, halo_c, rhs, back, stage_a, stage_b, cond,
    obs_sem, wts_sem, fac_sem, small_sem,
    halo_send, halo_recv, a_send, a_recv, b_send, b_recv,
):
    rows, rank, cols = fac.shape
    dates = obs.shape[2]
    per_row = cols // chunk
    steps = rows * per_row
    half = chunk // 2
    groups = n // group
    f32, bf16 = jnp.float32, jnp.bfloat16

    me = lax.axis_index("space")
    above = lax.rem(me + n - 1, n)
    below = lax.rem(me + 1, n)
    mine_a = lax.rem(me, group)
    mine_b = me // group
    peers_a = [mine_b * group + lax.rem(mine_a + k, group) for k in range(1, group)]
    peers_b = [lax.rem(mine_b + k, groups) * group + mine_a for k in range(1, groups)]

    barrier = pltpu.get_barrier_semaphore()
    greeted = [above, below] + peers_a + peers_b
    for peer in greeted:
        pl.semaphore_signal(
            barrier, inc=1, device_id={"space": peer}, device_id_type=pl.DeviceIdType.MESH
        )

    def chunk_copies(y, c, step):
        at = pl.ds(pl.multiple_of(c * chunk, chunk), chunk)
        return (
            pltpu.make_async_copy(obs_hbm.at[y, at], obs.at[y, at], obs_sem.at[step]),
            pltpu.make_async_copy(wts_hbm.at[y, at], wts.at[y, at], wts_sem.at[step]),
        )

    df_copy = pltpu.make_async_copy(df_hbm, df_ref, small_sem.at[2])
    db_copy = pltpu.make_async_copy(db_hbm, db_ref, small_sem.at[3])
    cond_copy = pltpu.make_async_copy(cond_hbm, cond_ref, small_sem.at[4])
    pb_copy = pltpu.make_async_copy(pb_hbm, pb, small_sem.at[0])
    lc_copy = pltpu.make_async_copy(lc_hbm, lc, small_sem.at[1])
    fac_copies = [
        pltpu.make_async_copy(fac_hbm.at[y], fac.at[y], fac_sem.at[y]) for y in range(rows)
    ]
    df_copy.start()
    db_copy.start()
    pb_copy.start()
    fac_copies[0].start()
    for y in range(rows):
        for c in range(per_row):
            for copy in chunk_copies(y, c, y * per_row + c):
                copy.start()
        if y + 1 < rows:
            fac_copies[y + 1].start()
    lc_copy.start()
    cond_copy.start()

    df_copy.wait()
    db_copy.wait()
    dh, dl = split(df_ref[...])
    bh, bl = split(db_ref[...])
    line = lax.broadcasted_iota(jnp.int32, (16, dates), 0)
    tail = jnp.where(
        line < 2, 1.0,
        jnp.where(line == 2, bh.astype(f32), jnp.where(line == 3, bl.astype(f32), 0.0)),
    ).astype(bf16)
    one = jnp.concatenate([dh, dh, dl, tail], axis=0)
    none = jnp.zeros_like(one)
    rhs[...] = jnp.concatenate(
        [jnp.concatenate([one, none], axis=1), jnp.concatenate([none, one], axis=1)], axis=0
    )
    ones_line = jnp.where(line == 0, 1.0, 0.0).astype(bf16)
    back[...] = jnp.concatenate(
        [
            jnp.concatenate([dh, dh], axis=1),
            jnp.concatenate([dl, jnp.zeros_like(dl)], axis=1),
            jnp.concatenate([ones_line, ones_line], axis=1),
        ],
        axis=0,
    )

    pl.semaphore_wait(barrier, len(greeted))

    def remote(src, dst, send, recv, peer):
        return pltpu.make_async_remote_copy(
            src_ref=src, dst_ref=dst, send_sem=send, recv_sem=recv,
            device_id={"space": peer}, device_id_type=pl.DeviceIdType.MESH,
        )

    halo = [
        remote(fac_hbm.at[0], halo_f.at[1], halo_send.at[0], halo_recv.at[0], above),
        remote(fac_hbm.at[rows - 1], halo_f.at[0], halo_send.at[1], halo_recv.at[1], below),
        remote(lc_hbm, halo_c.at[1], halo_send.at[2], halo_recv.at[2], above),
        remote(lc_hbm, halo_c.at[0], halo_send.at[3], halo_recv.at[3], below),
    ]
    for copy in halo:
        copy.start()
    pb_copy.wait()

    slot = lax.broadcasted_iota(jnp.int32, (16, chunk), 0)

    def body(y, c, carry):
        total, count = carry
        step = y * per_row + c
        for copy in chunk_copies(y, c, step):
            copy.wait()
        start = pl.multiple_of(c * chunk, chunk)
        fh, fl = split(fac[y, :, pl.ds(start, chunk)])
        ph, plow = split(pb[pl.ds(y, 1), pl.ds(start, chunk)])
        extra = jnp.where(
            slot == 0, ph.astype(f32),
            jnp.where(slot == 1, plow.astype(f32), jnp.where(slot < 4, 1.0, 0.0)),
        ).astype(bf16)
        lhs = jnp.concatenate([fh, fl, fh, extra], axis=0)
        halves = [lhs[:, :half], lhs[:, half:]]
        pred = lax.dot_general(
            jnp.concatenate(halves, axis=0), rhs[...], (((0,), (0,)), ((), ())),
            preferred_element_type=f32,
        )
        for j in range(2):
            at = pl.ds(pl.multiple_of(start + j * half, half), half)
            w = wts[y, at, :].astype(f32)
            count = count + jnp.sum(w.reshape(half // 8, 8, dates), axis=0)
            misfit = w * (pred[:, j * dates : (j + 1) * dates] - obs[y, at, :].astype(f32))
            mh, ml = split(misfit)
            both = jnp.concatenate([mh, ml], axis=1)
            total = total + lax.dot_general(
                halves[j], both, (((1,), (0,)), ((), ())), preferred_element_type=f32
            )
            pix = lax.dot_general(
                back[...], both, (((1,), (1,)), ((), ())), preferred_element_type=f32
            )
            gpf_ref[y, :, at] = pix[:rank] + pix[rank : 2 * rank]
            gpb_ref[pl.ds(y, 1), at] = pix[2 * rank : 2 * rank + 1]
        return total, count

    carry = (jnp.zeros((64, 2 * dates), f32), jnp.zeros((8, dates), f32))
    for y in range(rows):
        fac_copies[y].wait()
        carry = lax.fori_loop(0, per_row, functools.partial(body, y), carry)
    total, count = carry

    gdf = total[:rank, :dates] + total[:rank, dates:] + total[rank : 2 * rank, :dates]
    gdb = total[50:51, :dates] + total[50:51, dates:]
    line8 = lax.broadcasted_iota(jnp.int32, (8, dates), 0)
    last = jnp.where(
        line8 == 0, gdb, jnp.where(line8 == 1, jnp.sum(count, axis=0, keepdims=True), 0.0)
    )
    stage_a[mine_a] = jnp.concatenate([gdf, last], axis=0)
    sends_a = [
        remote(stage_a.at[mine_a], stage_a.at[mine_a], a_send.at[k], a_recv.at[k], peer)
        for k, peer in enumerate(peers_a)
    ]
    for copy in sends_a:
        copy.start()

    lc_copy.wait()
    cond_copy.wait()
    for copy in halo:
        copy.wait()
    cond[0:1] = jnp.where(me == 0, 0.0, lookup(halo_c[0, rows - 1 : rows, :], cond_ref))
    cond[rows + 1 : rows + 2] = jnp.where(me == n - 1, 0.0, lookup(halo_c[1, 0:1, :], cond_ref))
    cond[1 : rows + 1] = lookup(lc[...], cond_ref)

    def row_factors(y):
        return halo_f[0] if y < 0 else halo_f[1] if y == rows else fac[y]

    def smooth_row(y):
        own = cond[y + 1 : y + 2]
        north, south = cond[y : y + 1], cond[y + 2 : y + 3]
        f = fac[y]
        around = north + south + beside(own)
        weighted = north * row_factors(y - 1) + south * row_factors(y + 1) + beside(own * f)
        smooth[y] = own * (around * f - weighted)

    for y in range(rows // 2):
        smooth_row(y)

    for copy in sends_a:
        copy.wait()
    part = stage_a[0]
    for k in range(1, group):
        part = part + stage_a[k]
    stage_b[mine_b] = part
    sends_b = [
        remote(stage_b.at[mine_b], stage_b.at[mine_b], b_send.at[k], b_recv.at[k], peer)
        for k, peer in enumerate(peers_b)
    ]
    for copy in sends_b:
        copy.start()

    for y in range(rows // 2, rows):
        smooth_row(y)

    for copy in sends_b:
        copy.wait()
    part = stage_b[0]
    for k in range(1, groups):
        part = part + stage_b[k]
    clear = jnp.sum(part[rank + 1 : rank + 2], axis=1, keepdims=True)
    scale = jnp.float32(n * rows * cols) / clear
    gdf_ref[...] = scale * part[:rank]
    gdb_ref[...] = scale * part[rank : rank + 1]
    gpb_ref[...] = scale * gpb_ref[...]
    for y in range(rows):
        gpf_ref[y] = scale * gpf_ref[y] + smooth[y]


def place(*refs):
    half = len(refs) // 2
    sem = refs[-1]
    copies = [
        pltpu.make_async_copy(refs[i], refs[half + i], sem.at[i]) for i in range(half)
    ]
    for copy in copies:
        copy.start()
    for copy in copies:
        copy.wait()


def on_device(
    observed, weights, pixel_factors, pixel_bias, date_factors, date_bias, land_class, conductance
):
    rows, rank, cols = pixel_factors.shape
    dates = observed.shape[2]
    n = lax.axis_size("space")
    group = max(d for d in range(1, n + 1) if n % d == 0 and d * d <= n)
    groups = n // group
    chunk = min(CHUNK, cols)
    steps = rows * (cols // chunk)
    f32, bf16 = jnp.float32, jnp.bfloat16
    dma = pltpu.SemaphoreType.DMA
    anywhere = pl.BlockSpec(memory_space=pl.ANY)
    vmem = pl.BlockSpec(memory_space=pltpu.VMEM)
    shapes = (
        jax.ShapeDtypeStruct((rows, rank, cols), f32),
        jax.ShapeDtypeStruct((rows, cols), f32),
        jax.ShapeDtypeStruct((rank, dates), f32),
        jax.ShapeDtypeStruct((1, dates), f32),
    )
    grads = pl.pallas_call(
        functools.partial(kernel, n, group, chunk),
        out_shape=tuple(pltpu.VMEM(x.shape, x.dtype) for x in shapes),
        in_specs=[anywhere] * 8,
        out_specs=(vmem,) * 4,
        scratch_shapes=[
            pltpu.SMEM((CLASSES,), f32),
            pltpu.VMEM((rank, dates), f32),
            pltpu.VMEM((1, dates), f32),
            pltpu.VMEM((rows, cols, dates), bf16),
            pltpu.VMEM((rows, cols, dates), bf16),
            pltpu.VMEM((rows, rank, cols), f32),
            pltpu.VMEM((rows, cols), f32),
            pltpu.VMEM((rows, cols), jnp.int32),
            pltpu.VMEM((rows, rank, cols), f32),
            pltpu.VMEM((2, rank, cols), f32),
            pltpu.VMEM((2, rows, cols), jnp.int32),
            pltpu.VMEM((128, 2 * dates), bf16),
            pltpu.VMEM((48, 2 * dates), bf16),
            pltpu.VMEM((group, 24, dates), f32),
            pltpu.VMEM((groups, 24, dates), f32),
            pltpu.VMEM((rows + 2, cols), f32),
            dma((steps,)), dma((steps,)), dma((rows,)), dma((5,)),
            dma((4,)), dma((4,)),
            dma((group,)), dma((group,)), dma((groups,)), dma((groups,)),
        ],
        compiler_params=pltpu.CompilerParams(
            collective_id=0, has_side_effects=True, vmem_limit_bytes=GRANT
        ),
        name="gap_fill",
    )(
        *(
            pltpu.with_memory_space_constraint(x, pltpu.HBM)
            for x in (
                conductance, observed, weights, pixel_factors, pixel_bias, date_factors,
                date_bias.reshape(1, dates), land_class,
            )
        )
    )
    gpf, gpb, gdf, gdb = pl.pallas_call(
        place,
        out_shape=shapes,
        in_specs=[vmem] * 4,
        out_specs=(anywhere,) * 4,
        scratch_shapes=[dma((4,))],
        compiler_params=pltpu.CompilerParams(vmem_limit_bytes=4 * 1024 * 1024),
        name="place",
    )(*grads)
    return gpf, gpb, gdf, gdb.reshape(dates)


def solution(mesh):
    return jax.shard_map(
        on_device,
        mesh=mesh,
        in_specs=(
            P(("parts", "space"), None, None),
            P(("parts", "space"), None, None),
            P(("parts", "space"), None, None),
            P(("parts", "space"), None),
            P("parts", None),
            P("parts"),
            P(("parts", "space"), None),
            P(),
        ),
        out_specs=(
            P(("parts", "space"), None, None),
            P(("parts", "space"), None),
            P("parts", None),
            P("parts"),
        ),
        check_vma=False,
    )
```

```python
import functools

import jax
import jax.numpy as jnp
from jax import lax
from jax.experimental import pallas as pl
from jax.experimental.pallas import tpu as pltpu
from jax.sharding import PartitionSpec as P

CLASSES = 4
CHUNK = 4096
GRANT = 44 * 1024 * 1024


def split(x):
    head = x.astype(jnp.bfloat16)
    return head, (x - head.astype(jnp.float32)).astype(jnp.bfloat16)


def lookup(land_class, cond_ref):
    cond = jnp.zeros(land_class.shape, jnp.float32)
    for klass in range(CLASSES):
        cond = cond + jnp.where(land_class == klass, cond_ref[klass], jnp.float32(0.0))
    return cond


def beside(x):
    cols = x.shape[1]
    col = lax.broadcasted_iota(jnp.int32, x.shape, 1)
    left = jnp.where(col == 0, 0.0, pltpu.roll(x, 1, 1))
    right = jnp.where(col == cols - 1, 0.0, pltpu.roll(x, cols - 1, 1))
    return left + right


def kernel(
    n, group, chunk,
    cond_hbm, obs_hbm, wts_hbm, fac_hbm, pb_hbm, df_hbm, db_hbm, lc_hbm,
    gpf_ref, gpb_ref, gdf_ref, gdb_ref,
    cond_ref, df_ref, db_ref,
    obs, wts, fac, pb, lc, smooth, halo_f, halo_c, edge_c, rhs, back, stage_a, stage_b, cond,
    obs_sem, wts_sem, fac_sem, small_sem,
    halo_send, halo_recv, a_send, a_recv, b_send, b_recv,
):
    rows, rank, cols = fac.shape
    dates = obs.shape[2]
    per_row = cols // chunk
    steps = rows * per_row
    groups = n // group
    f32, bf16 = jnp.float32, jnp.bfloat16

    me = lax.axis_index("space")
    above = lax.rem(me + n - 1, n)
    below = lax.rem(me + 1, n)
    mine_a = lax.rem(me, group)
    mine_b = me // group
    peers_a = [mine_b * group + lax.rem(mine_a + k, group) for k in range(1, group)]
    peers_b = [lax.rem(mine_b + k, groups) * group + mine_a for k in range(1, groups)]

    barrier = pltpu.get_barrier_semaphore()
    greeted = [above, below] + peers_a + peers_b
    for peer in greeted:
        pl.semaphore_signal(
            barrier, inc=1, device_id={"space": peer}, device_id_type=pl.DeviceIdType.MESH
        )

    def chunk_copies(y, c, step):
        at = pl.ds(pl.multiple_of(c * chunk, chunk), chunk)
        return (
            pltpu.make_async_copy(obs_hbm.at[y, at], obs.at[y, at], obs_sem.at[step]),
            pltpu.make_async_copy(wts_hbm.at[y, at], wts.at[y, at], wts_sem.at[step]),
        )

    df_copy = pltpu.make_async_copy(df_hbm, df_ref, small_sem.at[2])
    db_copy = pltpu.make_async_copy(db_hbm, db_ref, small_sem.at[3])
    cond_copy = pltpu.make_async_copy(cond_hbm, cond_ref, small_sem.at[4])
    pb_copy = pltpu.make_async_copy(pb_hbm, pb, small_sem.at[0])
    lc_copy = pltpu.make_async_copy(lc_hbm, lc, small_sem.at[1])
    fac_copies = [
        pltpu.make_async_copy(fac_hbm.at[y], fac.at[y], fac_sem.at[y]) for y in range(rows)
    ]
    df_copy.start()
    db_copy.start()
    pb_copy.start()
    fac_copies[0].start()
    for y in range(rows):
        for c in range(per_row):
            for copy in chunk_copies(y, c, y * per_row + c):
                copy.start()
        if y + 1 < rows:
            fac_copies[y + 1].start()
    lc_copy.start()
    cond_copy.start()

    df_copy.wait()
    db_copy.wait()
    dh, dl = split(df_ref[...])
    bh, bl = split(db_ref[...])
    line = lax.broadcasted_iota(jnp.int32, (16, dates), 0)
    tail = jnp.where(
        line < 2, 1.0,
        jnp.where(line == 2, bh.astype(f32), jnp.where(line == 3, bl.astype(f32), 0.0)),
    ).astype(bf16)
    one = jnp.concatenate([dh, dh, dl, tail], axis=0)
    none = jnp.zeros_like(one)
    rhs[...] = jnp.concatenate(
        [jnp.concatenate([one, none], axis=1), jnp.concatenate([none, one], axis=1)], axis=0
    )
    ones_line = jnp.where(line == 0, 1.0, 0.0).astype(bf16)
    back[...] = jnp.concatenate(
        [
            jnp.concatenate([dh, dh], axis=1),
            jnp.concatenate([dl, jnp.zeros_like(dl)], axis=1),
            jnp.concatenate([ones_line, ones_line], axis=1),
        ],
        axis=0,
    )

    pl.semaphore_wait(barrier, len(greeted))

    def remote(src, dst, send, recv, peer):
        return pltpu.make_async_remote_copy(
            src_ref=src, dst_ref=dst, send_sem=send, recv_sem=recv,
            device_id={"space": peer}, device_id_type=pl.DeviceIdType.MESH,
        )

    halo = [
        remote(fac_hbm.at[0], halo_f.at[1], halo_send.at[0], halo_recv.at[0], above),
        remote(fac_hbm.at[rows - 1], halo_f.at[0], halo_send.at[1], halo_recv.at[1], below),
        remote(edge_c.at[0], halo_c.at[1], halo_send.at[2], halo_recv.at[2], above),
        remote(edge_c.at[1], halo_c.at[0], halo_send.at[3], halo_recv.at[3], below),
    ]
    for copy in halo[:2]:
        copy.start()
    pb_copy.wait()

    slot = lax.broadcasted_iota(jnp.int32, (16, chunk), 0)

    def operand(y, at):
        fh, fl = split(fac[y, :, at])
        ph, plow = split(pb[y : y + 1, at])
        extra = jnp.where(
            slot == 0, ph.astype(f32),
            jnp.where(slot == 1, plow.astype(f32), jnp.where(slot < 4, 1.0, 0.0)),
        ).astype(bf16)
        return jnp.concatenate([fh, fl, fh, extra], axis=0)

    def body(pair, c, carry):
        total, count = carry
        for y in pair:
            for copy in chunk_copies(y, c, y * per_row + c):
                copy.wait()
        at = pl.ds(pl.multiple_of(c * chunk, chunk), chunk)
        lhs = [operand(y, at) for y in pair]
        pred = lax.dot_general(
            jnp.concatenate(lhs, axis=0), rhs[...], (((0,), (0,)), ((), ())),
            preferred_element_type=f32,
        )
        for j, y in enumerate(pair):
            w = wts[y, at, :].astype(f32)
            count = count + jnp.sum(w.reshape(chunk // 8, 8, dates), axis=0)
            misfit = w * (pred[:, j * dates : (j + 1) * dates] - obs[y, at, :].astype(f32))
            mh, ml = split(misfit)
            both = jnp.concatenate([mh, ml], axis=1)
            total = total + lax.dot_general(
                lhs[j], both, (((1,), (0,)), ((), ())), preferred_element_type=f32
            )
            pix = lax.dot_general(
                back[...], both, (((1,), (1,)), ((), ())), preferred_element_type=f32
            )
            gpf_ref[y, :, at] = pix[:rank] + pix[rank : 2 * rank]
            gpb_ref[y : y + 1, at] = pix[2 * rank : 2 * rank + 1]
        return total, count

    carry = (jnp.zeros((64, 2 * dates), f32), jnp.zeros((8, dates), f32))
    for y in range(0, rows, 2):
        fac_copies[y].wait()
        fac_copies[y + 1].wait()
        carry = lax.fori_loop(0, per_row, functools.partial(body, (y, y + 1)), carry)
        if y == 0:
            lc_copy.wait()
            cond_copy.wait()
            cond[1 : rows + 1] = lookup(lc[...], cond_ref)
            edge_c[0] = cond[1:2]
            edge_c[1] = cond[rows : rows + 1]
            for copy in halo[2:]:
                copy.start()
    total, count = carry

    gdf = total[:rank, :dates] + total[:rank, dates:] + total[rank : 2 * rank, :dates]
    gdb = total[50:51, :dates] + total[50:51, dates:]
    line8 = lax.broadcasted_iota(jnp.int32, (8, dates), 0)
    last = jnp.where(
        line8 == 0, gdb, jnp.where(line8 == 1, jnp.sum(count, axis=0, keepdims=True), 0.0)
    )
    stage_a[mine_a] = jnp.concatenate([gdf, last], axis=0)
    sends_a = [
        remote(stage_a.at[mine_a], stage_a.at[mine_a], a_send.at[k], a_recv.at[k], peer)
        for k, peer in enumerate(peers_a)
    ]
    for copy in sends_a:
        copy.start()

    for copy in halo:
        copy.wait()
    cond[0:1] = jnp.where(me == 0, 0.0, halo_c[0])
    cond[rows + 1 : rows + 2] = jnp.where(me == n - 1, 0.0, halo_c[1])

    def row_factors(y):
        return halo_f[0] if y < 0 else halo_f[1] if y == rows else fac[y]

    def smooth_row(y):
        own = cond[y + 1 : y + 2]
        north, south = cond[y : y + 1], cond[y + 2 : y + 3]
        f = fac[y]
        around = north + south + beside(own)
        weighted = north * row_factors(y - 1) + south * row_factors(y + 1) + beside(own * f)
        smooth[y] = own * (around * f - weighted)

    for y in range(rows // 2):
        smooth_row(y)

    for copy in sends_a:
        copy.wait()
    part = stage_a[0]
    for k in range(1, group):
        part = part + stage_a[k]
    stage_b[mine_b] = part
    sends_b = [
        remote(stage_b.at[mine_b], stage_b.at[mine_b], b_send.at[k], b_recv.at[k], peer)
        for k, peer in enumerate(peers_b)
    ]
    for copy in sends_b:
        copy.start()

    for y in range(rows // 2, rows):
        smooth_row(y)

    for copy in sends_b:
        copy.wait()
    part = stage_b[0]
    for k in range(1, groups):
        part = part + stage_b[k]
    clear = jnp.sum(part[rank + 1 : rank + 2], axis=1, keepdims=True)
    scale = jnp.float32(n * rows * cols) / clear
    gdf_ref[...] = scale * part[:rank]
    gdb_ref[...] = scale * part[rank : rank + 1]
    gpb_ref[...] = scale * gpb_ref[...]
    for y in range(rows):
        gpf_ref[y] = scale * gpf_ref[y] + smooth[y]


def place(*refs):
    half = len(refs) // 2
    sem = refs[-1]
    copies = [
        pltpu.make_async_copy(refs[i], refs[half + i], sem.at[i]) for i in range(half)
    ]
    for copy in copies:
        copy.start()
    for copy in copies:
        copy.wait()


def on_device(
    observed, weights, pixel_factors, pixel_bias, date_factors, date_bias, land_class, conductance
):
    rows, rank, cols = pixel_factors.shape
    dates = observed.shape[2]
    n = lax.axis_size("space")
    group = max(d for d in range(1, n + 1) if n % d == 0 and d * d <= n)
    groups = n // group
    chunk = min(CHUNK, cols)
    steps = rows * (cols // chunk)
    f32, bf16 = jnp.float32, jnp.bfloat16
    dma = pltpu.SemaphoreType.DMA
    anywhere = pl.BlockSpec(memory_space=pl.ANY)
    vmem = pl.BlockSpec(memory_space=pltpu.VMEM)
    shapes = (
        jax.ShapeDtypeStruct((rows, rank, cols), f32),
        jax.ShapeDtypeStruct((rows, cols), f32),
        jax.ShapeDtypeStruct((rank, dates), f32),
        jax.ShapeDtypeStruct((1, dates), f32),
    )
    grads = pl.pallas_call(
        functools.partial(kernel, n, group, chunk),
        out_shape=tuple(pltpu.VMEM(x.shape, x.dtype) for x in shapes),
        in_specs=[anywhere] * 8,
        out_specs=(vmem,) * 4,
        scratch_shapes=[
            pltpu.SMEM((CLASSES,), f32),
            pltpu.VMEM((rank, dates), f32),
            pltpu.VMEM((1, dates), f32),
            pltpu.VMEM((rows, cols, dates), bf16),
            pltpu.VMEM((rows, cols, dates), bf16),
            pltpu.VMEM((rows, rank, cols), f32),
            pltpu.VMEM((rows, cols), f32),
            pltpu.VMEM((rows, cols), jnp.int32),
            pltpu.VMEM((rows, rank, cols), f32),
            pltpu.VMEM((2, rank, cols), f32),
            pltpu.VMEM((2, 1, cols), f32),
            pltpu.VMEM((2, 1, cols), f32),
            pltpu.VMEM((128, 2 * dates), bf16),
            pltpu.VMEM((48, 2 * dates), bf16),
            pltpu.VMEM((group, 24, dates), f32),
            pltpu.VMEM((groups, 24, dates), f32),
            pltpu.VMEM((rows + 2, cols), f32),
            dma((steps,)), dma((steps,)), dma((rows,)), dma((5,)),
            dma((4,)), dma((4,)),
            dma((group,)), dma((group,)), dma((groups,)), dma((groups,)),
        ],
        compiler_params=pltpu.CompilerParams(
            collective_id=0, has_side_effects=True, vmem_limit_bytes=GRANT
        ),
        name="gap_fill",
    )(
        *(
            pltpu.with_memory_space_constraint(x, pltpu.HBM)
            for x in (
                conductance, observed, weights, pixel_factors, pixel_bias, date_factors,
                date_bias.reshape(1, dates), land_class,
            )
        )
    )
    gpf, gpb, gdf, gdb = pl.pallas_call(
        place,
        out_shape=shapes,
        in_specs=[vmem] * 4,
        out_specs=(anywhere,) * 4,
        scratch_shapes=[dma((4,))],
        compiler_params=pltpu.CompilerParams(vmem_limit_bytes=4 * 1024 * 1024),
        name="place",
    )(*grads)
    return gpf, gpb, gdf, gdb.reshape(dates)


def solution(mesh):
    return jax.shard_map(
        on_device,
        mesh=mesh,
        in_specs=(
            P(("parts", "space"), None, None),
            P(("parts", "space"), None, None),
            P(("parts", "space"), None, None),
            P(("parts", "space"), None),
            P("parts", None),
            P("parts"),
            P(("parts", "space"), None),
            P(),
        ),
        out_specs=(
            P(("parts", "space"), None, None),
            P(("parts", "space"), None),
            P("parts", None),
            P("parts"),
        ),
        check_vma=False,
    )
```
